32 devices in a mesh: mp: 2 (over core), feat: 16 (over z, y, x).
Axes of the slice: x: 2, y: 2, z: 4, core: 2. Of those that a mesh axis runs over, the one named last changes fastest.
Arguments:
- residual: bfloat16 [2, 96, 2304], P(None, 'feat', 'mp'), may hold values from -6 to 6
- norm_gain: float32 [2, 2304], P(None, 'mp'), may hold values from 0.1 to 1.9
- gate_weight: bfloat16 [2, 2304, 9216], P(None, 'mp', 'feat'), may hold values from -0.125 to 0.125
- up_weight: bfloat16 [2, 2304, 9216], P(None, 'mp', 'feat'), may hold values from -0.125 to 0.125
- down_weight: bfloat16 [2, 9216, 2304], P(None, 'feat', 'mp'), may hold values from -0.0625 to 0.0625
- encoder: bfloat16 [2, 32768, 2304], P(None, 'feat', 'mp'), may hold values from -0.125 to 0.125
- encoder_bias: float32 [2, 32768], P(None, 'feat'), may hold values from -3 to 3
- decoder: bfloat16 [3, 32768, 2304], P(None, 'feat', 'mp'), may hold values from -0.03125 to 0.03125
Outputs:
- grad_encoder: bfloat16 [2, 32768, 2304], P(None, 'feat', 'mp')
- grad_bias: float32 [2, 32768], P(None, 'feat')
- grad_decoder: bfloat16 [3, 32768, 2304], P(None, 'feat', 'mp')
The draws below stay inside these ranges and needn't reach their ends.
All inputs are finite; a program needn't handle non-finite values.
Results may differ from the reference program's by a relative error of at most 0.02.
The reference program's roundings to bfloat16 on the way count: a program that leaves them out, or rounds other values in their place, can miss the bound.
Values may be sent and summed in bfloat16 or wider, within the bound.
No kernel may reach another device: no remote copies, remote signals or barrier semaphores. Data moves between devices by JAX's collectives and lax.ppermute only.
A program may use at most 128 MiB of HBM per device.

```python
import math
import jax
import jax.numpy as jnp
from jax import lax

D = 2304
FF = 9216
F = 32768
TOKENS = 96


def steps_of(rng, dims, pieces, smallest, top_value):
    def one(axis_at, shards_of):
        draws = jax.random.uniform(jax.random.fold_in(jax.random.fold_in(rng, 6), axis_at), (shards_of,), jnp.float32, smallest / len(pieces), top_value / len(pieces))
        return jnp.repeat(jnp.exp(draws), dims[axis_at] // shards_of).reshape((-1,) + (1,) * (len(dims) - axis_at - 1))

    loudness = one(*pieces[0])
    for cut in pieces[1:]:
        loudness = loudness * one(*cut)
    return loudness


def gaussian(rng, shape, deviation, limit, pieces=(), held_as=jnp.bfloat16):
    drawn = deviation * jax.random.normal(rng, shape, jnp.float32)
    if pieces:
        drawn = drawn * steps_of(rng, shape, pieces, -0.22, 0.18)
    return jnp.clip(drawn, -limit, limit).astype(held_as)


def setup_inputs(seed: int = 0) -> dict:
    keys = jax.random.split(jax.random.key(seed), 9)
    residual = gaussian(keys[0], (2, TOKENS, D), 1.0, 6.0, ((1, 16), (2, 2)))
    norm_gain = jnp.clip(1.0 + 0.18 * jax.random.normal(keys[1], (2, D), jnp.float32), 0.1, 1.9)
    gate_weight = gaussian(keys[2], (2, D, FF), D ** -0.5, 0.125, ((1, 2), (2, 16)))
    up_weight = gaussian(keys[3], (2, D, FF), D ** -0.5, 0.125, ((1, 2), (2, 16)))
    down_weight = gaussian(keys[4], (2, FF, D), FF ** -0.5, 0.0625, ((1, 16), (2, 2)))
    encoder = gaussian(keys[5], (2, F, D), D ** -0.5, 0.125, ((1, 16), (2, 2)))
    encoder_bias = gaussian(keys[6], (2, F), 0.5, 3.0, ((1, 16),), jnp.float32)
    decoder = gaussian(keys[7], (3, F, D), F ** -0.5, 0.03125, ((1, 16), (2, 2)))
    return dict(residual=residual, norm_gain=norm_gain, gate_weight=gate_weight, up_weight=up_weight, down_weight=down_weight, encoder=encoder, encoder_bias=encoder_bias, decoder=decoder)


sparsity_weight = 0.1

def outer_product(weights_side, errors_side):
    return jnp.dot(weights_side.T, errors_side, preferred_element_type=jnp.float32)

def reference(residual, norm_gain, gate_weight, up_weight, down_weight, encoder, encoder_bias, decoder):
    values = residual.astype(jnp.float32)
    mean_square = lax.optimization_barrier(jnp.mean(values * values, axis=2, keepdims=True))
    normed = (values * jax.lax.rsqrt(mean_square + 1e-06) * norm_gain[:, None, :]).astype(jnp.bfloat16)
    targets = []
    actives = []
    for layer_index in range(2):
        gate_part = jnp.dot(normed[layer_index], gate_weight[layer_index], preferred_element_type=jnp.float32)
        up_part = jnp.dot(normed[layer_index], up_weight[layer_index], preferred_element_type=jnp.float32)
        hidden = (jax.nn.gelu(gate_part, approximate=True) * up_part).astype(jnp.bfloat16)
        targets.append(jnp.dot(hidden, down_weight[layer_index], preferred_element_type=jnp.float32))
        preact = jnp.dot(normed[layer_index], encoder[layer_index].T, preferred_element_type=jnp.float32) + encoder_bias[layer_index][None, :]
        actives.append(jnp.maximum(preact, 0.0).astype(jnp.bfloat16))
    rebuilt_first = jnp.dot(actives[0], decoder[0], preferred_element_type=jnp.float32)
    rebuilt_second = jnp.dot(actives[0], decoder[1], preferred_element_type=jnp.float32) + jnp.dot(actives[1], decoder[2], preferred_element_type=jnp.float32)
    error_first = (rebuilt_first - targets[0]).astype(jnp.bfloat16)
    error_second = (rebuilt_second - targets[1]).astype(jnp.bfloat16)
    loss_scale = 1.0 / math.sqrt(TOKENS)
    back_first = jnp.dot(error_first, decoder[0].T, preferred_element_type=jnp.float32) + jnp.dot(error_second, decoder[1].T, preferred_element_type=jnp.float32)
    back_second = jnp.dot(error_second, decoder[2].T, preferred_element_type=jnp.float32)
    grad_first = jnp.where(actives[0] > 0, loss_scale * (back_first + sparsity_weight), 0.0).astype(jnp.bfloat16)
    grad_second = jnp.where(actives[1] > 0, loss_scale * (back_second + sparsity_weight), 0.0).astype(jnp.bfloat16)
    grad_encoder = jnp.stack([outer_product(grad_first, normed[0]), outer_product(grad_second, normed[1])]).astype(jnp.bfloat16)
    grad_bias = jnp.stack([lax.optimization_barrier(jnp.sum(grad_first.astype(jnp.float32), axis=0)), lax.optimization_barrier(jnp.sum(grad_second.astype(jnp.float32), axis=0))])
    grad_decoder = (loss_scale * jnp.stack([outer_product(actives[0], error_first), outer_product(actives[0], error_second), outer_product(actives[1], error_second)])).astype(jnp.bfloat16)
    return (grad_encoder, grad_bias, grad_decoder)
```

```python
import math

import jax
import jax.numpy as jnp
from jax import lax
from jax.sharding import PartitionSpec as P

D = 2304


sparsity_weight = 0.1


def swap(values, axis, bit):
    size = lax.axis_size(axis)
    return lax.ppermute(values, axis, [(i, i ^ bit) for i in range(size)])


def bits_of(axis):
    size = lax.axis_size(axis)
    return [1 << k for k in range(size.bit_length() - 1)]


def mp_sum(values, wire=None):
    for bit in bits_of("mp"):
        sent = values if wire is None else values.astype(wire)
        values = values + swap(sent, "mp", bit).astype(values.dtype)
    return values


def gather_tokens(values, dim):
    for bit in reversed(bits_of("feat")):
        values = jnp.concatenate([values, swap(values, "feat", bit)], axis=dim)
    return values


def scatter_tokens(values):
    for bit in bits_of("feat"):
        half = values.shape[0] // 2
        values = values[:half] + swap(values[half:].astype(jnp.bfloat16), "feat", bit).astype(jnp.float32)
    return values


def dot(a, b, contract):
    return lax.dot_general(a, b, (contract, ((), ())), preferred_element_type=jnp.float32)


def body(residual, norm_gain, gate_weight, up_weight, down_weight, encoder, encoder_bias, decoder):
    values = residual.astype(jnp.float32)
    squares = mp_sum(jnp.sum(values * values, axis=2))
    inverse_rms = lax.rsqrt(squares / D + 1e-06)
    normed_local = (values * inverse_rms[:, :, None] * norm_gain[:, None, :]).astype(jnp.bfloat16)
    normed = gather_tokens(normed_local, 1)
    tokens = normed.shape[1]
    gate_part = jnp.einsum("ltd,ldh->lth", normed, gate_weight, preferred_element_type=jnp.float32)
    up_part = jnp.einsum("ltd,ldh->lth", normed, up_weight, preferred_element_type=jnp.float32)
    mlp_part = mp_sum(jnp.stack([gate_part, up_part]).astype(jnp.bfloat16)).astype(jnp.float32)
    hidden = (jax.nn.gelu(mlp_part[0], approximate=True) * mlp_part[1]).astype(jnp.bfloat16)
    preact = mp_sum(
        jnp.einsum("ltd,lfd->ltf", normed, encoder, preferred_element_type=jnp.float32)
    )
    active = jnp.maximum(preact + encoder_bias[:, None, :], 0.0).astype(jnp.bfloat16)
    target = jnp.einsum("lth,lhd->ltd", hidden, down_weight, preferred_element_type=jnp.float32)
    model_cols = decoder.shape[2]
    nn = ((1,), (0,))
    nt = ((1,), (1,))
    first = dot(active[0], decoder[0], nn) - target[0]
    second = dot(active[0], decoder[1], nn) + dot(active[1], decoder[2], nn) - target[1]
    errors_local = scatter_tokens(jnp.concatenate([first, second], axis=1)).astype(jnp.bfloat16)
    errors = gather_tokens(errors_local, 0)
    error_first = errors[:, :model_cols]
    error_second = errors[:, model_cols:]
    back_first = dot(error_first, decoder[0], nt) + dot(error_second, decoder[1], nt)
    back_second = dot(error_second, decoder[2], nt)
    loss_scale = 1.0 / math.sqrt(tokens)
    backward = mp_sum(jnp.stack([back_first, back_second]).astype(jnp.bfloat16)).astype(jnp.float32)
    pre_grad = jnp.where(active > 0, loss_scale * (backward + sparsity_weight), 0.0).astype(
        jnp.bfloat16
    )
    grad_encoder = jnp.einsum(
        "ltf,ltd->lfd", pre_grad, normed, preferred_element_type=jnp.float32
    ).astype(jnp.bfloat16)
    grad_bias = jnp.sum(pre_grad.astype(jnp.float32), axis=1)
    grad_decoder = (
        loss_scale
        * jnp.einsum(
            "ltf,ltd->lfd",
            jnp.stack([active[0], active[0], active[1]]),
            jnp.stack([error_first, error_second, error_second]),
            preferred_element_type=jnp.float32,
        )
    ).astype(jnp.bfloat16)
    return (grad_encoder, grad_bias, grad_decoder)


def solution(mesh):
    return jax.shard_map(
        body,
        mesh=mesh,
        in_specs=(
            P(None, "feat", "mp"),
            P(None, "mp"),
            P(None, "mp", "feat"),
            P(None, "mp", "feat"),
            P(None, "feat", "mp"),
            P(None, "feat", "mp"),
            P(None, "feat"),
            P(None, "feat", "mp"),
        ),
        out_specs=(P(None, "feat", "mp"), P(None, "feat"), P(None, "feat", "mp")),
        check_vma=False,
    )
```

```python
import math

import jax
import jax.numpy as jnp
from jax import lax
from jax.experimental import pallas as pl
from jax.experimental.pallas import tpu as pltpu
from jax.sharding import PartitionSpec as P

D = 2304


sparsity_weight = 0.1


def swap(values, axis, bit):
    size = lax.axis_size(axis)
    return lax.ppermute(values, axis, [(i, i ^ bit) for i in range(size)])


def bits_of(axis):
    size = lax.axis_size(axis)
    return [1 << k for k in range(size.bit_length() - 1)]


def mp_sum(values, wire=None):
    for bit in bits_of("mp"):
        sent = values if wire is None else values.astype(wire)
        values = values + swap(sent, "mp", bit).astype(values.dtype)
    return values


def join(*parts):
    return jnp.concatenate(parts, axis=0)


def gather_inner(block):
    place = lax.axis_index("feat")
    for bit in reversed(bits_of("feat")[2:]):
        other = swap(block, "feat", bit)
        upper = (place & bit) > 0
        block = join(jnp.where(upper, other, block), jnp.where(upper, block, other))
    return block


def gather_outer(quarter, layer):
    rows = quarter.shape[0]
    if layer == 0:
        half = join(quarter, swap(quarter, "feat", 2))
        return join(half, swap(half, "feat", 1))
    across = swap(quarter, "feat", 1)
    other = swap(join(quarter, across), "feat", 2)
    return join(quarter, other[:rows], across, other[rows:])


def send_add(kept, sent, bit):
    return kept + swap(sent.astype(jnp.bfloat16), "feat", bit).astype(jnp.float32)


def scatter_outer(values, layer):
    rows = values.shape[0] // 4
    own, second, first, both = (values[k * rows : (k + 1) * rows] for k in range(4))
    if layer == 0:
        half = send_add(values[: 2 * rows], values[2 * rows :], 1)
        return send_add(half[:rows], half[rows:], 2)
    half = send_add(join(own, first), join(second, both), 2)
    return send_add(half[:rows], half[rows:], 1)


def sum_inner(quarter):
    bits = bits_of("feat")[2:]
    for bit in bits:
        received = swap(quarter.astype(jnp.bfloat16), "feat", bit)
        if bit == bits[-1]:
            return add_round(quarter, received, int(4e10))
        quarter = quarter + received.astype(jnp.float32)


def square_sums(values, flops):
    def kernel(values_ref, out_ref):
        v = values_ref[...].astype(jnp.float32)
        out_ref[...] = jnp.sum(v * v, axis=2)

    return pl.pallas_call(
        kernel,
        out_shape=jax.ShapeDtypeStruct(values.shape[:2], jnp.float32),
        in_specs=[pl.BlockSpec(memory_space=pltpu.VMEM)],
        out_specs=pl.BlockSpec(memory_space=pltpu.VMEM),
        compiler_params=pltpu.CompilerParams(vmem_limit_bytes=4 << 20),
        cost_estimate=pl.CostEstimate(flops=flops, bytes_accessed=1 << 16, transcendentals=0),
    )(values)


def add_round(kept, received, flops):
    def kernel(kept_ref, received_ref, out_ref):
        total = kept_ref[...] + received_ref[...].astype(jnp.float32)
        out_ref[...] = total.astype(jnp.bfloat16)

    return pl.pallas_call(
        kernel,
        out_shape=jax.ShapeDtypeStruct(kept.shape, jnp.bfloat16),
        in_specs=[pl.BlockSpec(memory_space=pltpu.VMEM)] * 2,
        out_specs=pl.BlockSpec(memory_space=pltpu.VMEM),
        compiler_params=pltpu.CompilerParams(vmem_limit_bytes=4 << 20),
        cost_estimate=pl.CostEstimate(flops=flops, bytes_accessed=1 << 16, transcendentals=0),
    )(kept, received)


def row_chunks(rows, most):
    size = min(rows, most)
    while rows % size:
        size //= 2
    return [(at, size) for at in range(0, rows, size)]


def dot(a, b, contract):
    return lax.dot_general(a, b, (contract, ((), ())), preferred_element_type=jnp.float32)


tn = ((0,), (0,))
nn = ((1,), (0,))
nt = ((1,), (1,))


def decoder_gradient(active, errors, scale):
    tokens, features = active[0].shape
    cols = errors[0].shape[1]
    picks = [(0, 0), (0, 1), (1, 1)]
    chunks = row_chunks(features, 256)

    def kernel(active_0, active_1, errors_0, errors_1, out_ref, held, sems):
        actives, error_refs = (active_0, active_1), (errors_0, errors_1)
        copies = []
        for k, (a, e) in enumerate(picks):
            right = error_refs[e][...]
            for c, (at, size) in enumerate(chunks):
                rows = pl.ds(at, size)
                held[k, rows] = (scale * dot(actives[a][:, rows], right, tn)).astype(jnp.bfloat16)
                copies.append(pltpu.make_async_copy(held.at[k, rows], out_ref.at[k, rows], sems.at[k, c]))
                copies[-1].start()
        for copy in copies:
            copy.wait()

    vmem = pl.BlockSpec(memory_space=pltpu.VMEM)
    return pl.pallas_call(
        kernel,
        out_shape=jax.ShapeDtypeStruct((3, features, cols), jnp.bfloat16),
        in_specs=[vmem] * 4,
        out_specs=pl.BlockSpec(memory_space=pl.ANY),
        scratch_shapes=[
            pltpu.VMEM((3, features, cols), jnp.bfloat16),
            pltpu.SemaphoreType.DMA((3, len(chunks))),
        ],
        compiler_params=pltpu.CompilerParams(vmem_limit_bytes=24 << 20),
        cost_estimate=pl.CostEstimate(
            flops=6 * tokens * features * cols, bytes_accessed=6 * features * cols, transcendentals=0
        ),
    )(*active, *errors)


def encoder_gradient(active, own, received, normed, scale):
    tokens, features = active[0].shape
    cols = normed[0].shape[1]
    chunks = row_chunks(features, 256)

    def kernel(active_0, active_1, own_ref, received_ref, normed_0, normed_1, out_ref, bias_ref, held, sems):
        copies = []
        for l, (active_ref, normed_ref) in enumerate(((active_0, normed_0), (active_1, normed_1))):
            right = normed_ref[...]
            for c, (at, size) in enumerate(chunks):
                rows = pl.ds(at, size)
                backward = own_ref[l, :, rows].astype(jnp.float32) + received_ref[l, :, rows].astype(jnp.float32)
                open_gate = active_ref[:, rows].astype(jnp.float32) > 0
                pre_grad = jnp.where(open_gate, scale * (backward + sparsity_weight), 0.0).astype(jnp.bfloat16)
                bias_ref[l : l + 1, rows] = jnp.sum(pre_grad.astype(jnp.float32), axis=0, keepdims=True)
                held[l, rows] = dot(pre_grad, right, tn).astype(jnp.bfloat16)
                copies.append(pltpu.make_async_copy(held.at[l, rows], out_ref.at[l, rows], sems.at[l, c]))
                copies[-1].start()
        for copy in copies:
            copy.wait()

    vmem = pl.BlockSpec(memory_space=pltpu.VMEM)
    return pl.pallas_call(
        kernel,
        out_shape=(
            jax.ShapeDtypeStruct((2, features, cols), jnp.bfloat16),
            jax.ShapeDtypeStruct((2, features), jnp.float32),
        ),
        in_specs=[vmem] * 6,
        out_specs=(pl.BlockSpec(memory_space=pl.ANY), vmem),
        scratch_shapes=[
            pltpu.VMEM((2, features, cols), jnp.bfloat16),
            pltpu.SemaphoreType.DMA((2, len(chunks))),
        ],
        compiler_params=pltpu.CompilerParams(vmem_limit_bytes=24 << 20),
        cost_estimate=pl.CostEstimate(
            flops=4 * tokens * features * cols, bytes_accessed=4 * features * cols, transcendentals=0
        ),
    )(*active, own, received, *normed)


def body(residual, norm_gain, gate_weight, up_weight, down_weight, encoder, encoder_bias, decoder):
    values = residual.astype(jnp.float32)
    squares = mp_sum(square_sums(residual, int(4e11)))
    inverse_rms = lax.rsqrt(squares / D + 1e-06)
    normed_local = (values * inverse_rms[:, :, None] * norm_gain[:, None, :]).astype(jnp.bfloat16)
    model_cols = decoder.shape[2]
    quarter = gather_inner(jnp.concatenate([normed_local[0], normed_local[1]], axis=1))
    normed = [gather_outer(quarter[:, l * model_cols : (l + 1) * model_cols], l) for l in range(2)]
    tokens = normed[0].shape[0]
    active = []
    target = []
    for l in range(2):
        preact = mp_sum(dot(normed[l], encoder[l], nt))
        active.append(jnp.maximum(preact + encoder_bias[l][None, :], 0.0).astype(jnp.bfloat16))
        gate_part = dot(normed[l], gate_weight[l], nn)
        up_part = dot(normed[l], up_weight[l], nn)
        mlp = mp_sum(jnp.stack([gate_part, up_part]).astype(jnp.bfloat16)).astype(jnp.float32)
        hidden = (jax.nn.gelu(mlp[0], approximate=True) * mlp[1]).astype(jnp.bfloat16)
        target.append(dot(hidden, down_weight[l], nn))
    partial = [
        dot(active[0], decoder[0], nn) - target[0],
        dot(active[0], decoder[1], nn) + dot(active[1], decoder[2], nn) - target[1],
    ]
    errors = [
        gather_outer(sum_inner(scatter_outer(partial[l], l)), l)
        for l in range(2)
    ]
    back_first = dot(errors[0], decoder[0], nt) + dot(errors[1], decoder[1], nt)
    back_second = dot(errors[1], decoder[2], nt)
    loss_scale = 1.0 / math.sqrt(tokens)
    own = jnp.stack([back_first, back_second]).astype(jnp.bfloat16)
    *inner, last = bits_of("mp")
    for bit in inner:
        own = own + swap(own, "mp", bit)
    received = swap(own, "mp", last)
    grad_decoder = decoder_gradient(active, errors, loss_scale)
    grad_encoder, grad_bias = encoder_gradient(active, own, received, normed, loss_scale)
    return (grad_encoder, grad_bias, grad_decoder)


def solution(mesh):
    return jax.shard_map(
        body,
        mesh=mesh,
        in_specs=(
            P(None, "feat", "mp"),
            P(None, "mp"),
            P(None, "mp", "feat"),
            P(None, "mp", "feat"),
            P(None, "feat", "mp"),
            P(None, "feat", "mp"),
            P(None, "feat"),
            P(None, "feat", "mp"),
        ),
        out_specs=(P(None, "feat", "mp"), P(None, "feat"), P(None, "feat", "mp")),
        check_vma=False,
    )
```

```python
import math

import jax
import jax.numpy as jnp
from jax import lax
from jax.experimental import pallas as pl
from jax.experimental.pallas import tpu as pltpu
from jax.sharding import PartitionSpec as P


D = 2304


sparsity_weight = 0.1


def swap(values, axis, bit):
    size = lax.axis_size(axis)
    return lax.ppermute(values, axis, [(i, i ^ bit) for i in range(size)])


def bits_of(axis):
    size = lax.axis_size(axis)
    return [1 << k for k in range(size.bit_length() - 1)]


def mp_sum(values):
    for bit in bits_of("mp"):
        values = values + swap(values, "mp", bit)
    return values


def join(*parts):
    return jnp.concatenate(parts, axis=0)


def gather_inner(block):
    place = lax.axis_index("feat")
    bits = bits_of("feat")[2:]
    if len(bits) != 2:
        for bit in reversed(bits):
            other = swap(block, "feat", bit)
            upper = (place & bit) > 0
            block = join(jnp.where(upper, other, block), jnp.where(upper, block, other))
        return block
    low, high = bits
    far, both, near = (swap(block, "feat", b) for b in (high, high | low, low))
    at_low, at_high = (place & low) > 0, (place & high) > 0

    def pick(l, h):
        same_low = jnp.where(at_high == h, block, far)
        other_low = jnp.where(at_high == h, near, both)
        return jnp.where(at_low == l, same_low, other_low)

    return join(pick(False, False), pick(False, True), pick(True, False), pick(True, True))


def stack_rows(upper, lower, flops):
    rows, cols = upper.shape

    def kernel(upper_ref, lower_ref, out_ref):
        out_ref[:rows] = upper_ref[...]
        out_ref[rows:] = lower_ref[...]

    return pl.pallas_call(
        kernel,
        out_shape=jax.ShapeDtypeStruct((2 * rows, cols), upper.dtype),
        in_specs=[pl.BlockSpec(memory_space=pltpu.VMEM)] * 2,
        out_specs=pl.BlockSpec(memory_space=pltpu.VMEM),
        compiler_params=pltpu.CompilerParams(vmem_limit_bytes=4 << 20),
        cost_estimate=pl.CostEstimate(flops=flops, bytes_accessed=1 << 16, transcendentals=0),
    )(upper, lower)


def gather_outer(quarter, layer, flops):
    rows = quarter.shape[0]
    near, far = ((2, 1), (1, 2))[layer]
    across = swap(quarter, "feat", near)
    half = stack_rows(quarter, across, flops) if flops else join(quarter, across)
    other = swap(half, "feat", far)
    if layer == 0:
        return join(half, other)
    return join(quarter, other[:rows], across, other[rows:])


def send_add(kept, sent, bit):
    return kept + swap(sent.astype(jnp.bfloat16), "feat", bit).astype(jnp.float32)


def sum_tokens(values, layer):
    rows = values.shape[0] // 4
    own, second, first, both = (values[k * rows : (k + 1) * rows] for k in range(4))
    if layer == 0:
        half = send_add(values[: 2 * rows], values[2 * rows :], 1)
        quarter = send_add(half[:rows], half[rows:], 2)
    else:
        half = send_add(join(own, first), join(second, both), 2)
        quarter = send_add(half[:rows], half[rows:], 1)
    bits = bits_of("feat")[2:]
    if len(bits) == 2:
        sent = quarter.astype(jnp.bfloat16)
        offsets = (bits[1], bits[0] | bits[1], bits[0])
        received = [swap(sent, "feat", b) for b in offsets]
        for other in received[:-1]:
            quarter = quarter + other.astype(jnp.float32)
        return add_round(quarter, received[-1], int(4e10))
    for bit in bits:
        received = swap(quarter.astype(jnp.bfloat16), "feat", bit)
        quarter = quarter + received.astype(jnp.float32)
    return quarter.astype(jnp.bfloat16)


def square_sums(values, flops):
    def kernel(values_ref, out_ref):
        v = values_ref[...].astype(jnp.float32)
        out_ref[...] = jnp.sum(v * v, axis=2)

    return pl.pallas_call(
        kernel,
        out_shape=jax.ShapeDtypeStruct(values.shape[:2], jnp.float32),
        in_specs=[pl.BlockSpec(memory_space=pltpu.VMEM)],
        out_specs=pl.BlockSpec(memory_space=pltpu.VMEM),
        compiler_params=pltpu.CompilerParams(vmem_limit_bytes=4 << 20),
        cost_estimate=pl.CostEstimate(flops=flops, bytes_accessed=1 << 16, transcendentals=0),
    )(values)


def add_round(kept, received, flops):
    def kernel(kept_ref, received_ref, out_ref):
        total = kept_ref[...] + received_ref[...].astype(jnp.float32)
        out_ref[...] = total.astype(jnp.bfloat16)

    return pl.pallas_call(
        kernel,
        out_shape=jax.ShapeDtypeStruct(kept.shape, jnp.bfloat16),
        in_specs=[pl.BlockSpec(memory_space=pltpu.VMEM)] * 2,
        out_specs=pl.BlockSpec(memory_space=pltpu.VMEM),
        compiler_params=pltpu.CompilerParams(vmem_limit_bytes=4 << 20),
        cost_estimate=pl.CostEstimate(flops=flops, bytes_accessed=1 << 16, transcendentals=0),
    )(kept, received)


def row_chunks(rows, most):
    size = min(rows, most)
    while rows % size:
        size //= 2
    return [(at, size) for at in range(0, rows, size)]


def dot(a, b, contract):
    return lax.dot_general(a, b, (contract, ((), ())), preferred_element_type=jnp.float32)


tn = ((0,), (0,))
nn = ((1,), (0,))
nt = ((1,), (1,))


def decoder_gradient(lefts, right, scale, slots, into=None):
    tokens, features = lefts[0].shape
    cols = right.shape[1]
    count = len(lefts)
    chunks = row_chunks(features, 256)

    def kernel(*refs):
        left_refs, right_ref = refs[:count], refs[count]
        out_ref, held, sems = refs[-3:]
        right_value = right_ref[...]
        copies = []
        for k, left_ref in enumerate(left_refs):
            for c, (at, size) in enumerate(chunks):
                rows = pl.ds(at, size)
                held[k, rows] = (scale * dot(left_ref[:, rows], right_value, tn)).astype(jnp.bfloat16)
                target = out_ref.at[slots[k], rows]
                copies.append(pltpu.make_async_copy(held.at[k, rows], target, sems.at[k, c]))
                copies[-1].start()
        for copy in copies:
            copy.wait()

    vmem = pl.BlockSpec(memory_space=pltpu.VMEM)
    hbm = pl.BlockSpec(memory_space=pl.ANY)
    more = () if into is None else (into,)
    return pl.pallas_call(
        kernel,
        out_shape=jax.ShapeDtypeStruct((3, features, cols), jnp.bfloat16),
        in_specs=[vmem] * (count + 1) + [hbm] * len(more),
        out_specs=hbm,
        input_output_aliases={count + 1: 0} if more else {},
        scratch_shapes=[
            pltpu.VMEM((count, features, cols), jnp.bfloat16),
            pltpu.SemaphoreType.DMA((count, len(chunks))),
        ],
        compiler_params=pltpu.CompilerParams(vmem_limit_bytes=(8 + 8 * count) << 20),
        cost_estimate=pl.CostEstimate(
            flops=2 * count * tokens * features * cols,
            bytes_accessed=2 * count * features * cols,
            transcendentals=0,
        ),
    )(*lefts, right, *more)


def encoder_gradient(active, own, received, normed, scale):
    tokens, features = active[0].shape
    cols = normed[0].shape[1]
    chunks = row_chunks(features, 256)

    def kernel(active_0, active_1, own_ref, received_ref, normed_0, normed_1, out_ref, bias_ref, held, sems):
        copies = []
        for l, (active_ref, normed_ref) in enumerate(((active_0, normed_0), (active_1, normed_1))):
            right = normed_ref[...]
            for c, (at, size) in enumerate(chunks):
                rows = pl.ds(at, size)
                backward = own_ref[l, :, rows].astype(jnp.float32) + received_ref[l, :, rows].astype(jnp.float32)
                open_gate = active_ref[:, rows].astype(jnp.float32) > 0
                pre_grad = jnp.where(open_gate, scale * (backward + sparsity_weight), 0.0).astype(jnp.bfloat16)
                bias_ref[l : l + 1, rows] = jnp.sum(pre_grad.astype(jnp.float32), axis=0, keepdims=True)
                held[l, rows] = dot(pre_grad, right, tn).astype(jnp.bfloat16)
                copies.append(pltpu.make_async_copy(held.at[l, rows], out_ref.at[l, rows], sems.at[l, c]))
                copies[-1].start()
        for copy in copies:
            copy.wait()

    vmem = pl.BlockSpec(memory_space=pltpu.VMEM)
    return pl.pallas_call(
        kernel,
        out_shape=(
            jax.ShapeDtypeStruct((2, features, cols), jnp.bfloat16),
            jax.ShapeDtypeStruct((2, features), jnp.float32),
        ),
        in_specs=[vmem] * 6,
        out_specs=(pl.BlockSpec(memory_space=pl.ANY), vmem),
        scratch_shapes=[
            pltpu.VMEM((2, features, cols), jnp.bfloat16),
            pltpu.SemaphoreType.DMA((2, len(chunks))),
        ],
        compiler_params=pltpu.CompilerParams(vmem_limit_bytes=24 << 20),
        cost_estimate=pl.CostEstimate(
            flops=4 * tokens * features * cols, bytes_accessed=4 * features * cols, transcendentals=0
        ),
    )(*active, own, received, *normed)


def body(residual, norm_gain, gate_weight, up_weight, down_weight, encoder, encoder_bias, decoder):
    values = residual.astype(jnp.float32)
    squares = mp_sum(square_sums(residual, int(4e11)))
    inverse_rms = lax.rsqrt(squares / D + 1e-06)
    normed_local = (values * inverse_rms[:, :, None] * norm_gain[:, None, :]).astype(jnp.bfloat16)
    model_cols = decoder.shape[2]
    quarter = gather_inner(jnp.concatenate([normed_local[0], normed_local[1]], axis=1))
    normed = [gather_outer(quarter[:, l * model_cols : (l + 1) * model_cols], l, int(4e10)) for l in range(2)]
    tokens = normed[0].shape[0]
    active = []
    target = []
    for l in range(2):
        preact = mp_sum(dot(normed[l], encoder[l], nt))
        active.append(jnp.maximum(preact + encoder_bias[l][None, :], 0.0).astype(jnp.bfloat16))
        gate_part = dot(normed[l], gate_weight[l], nn)
        up_part = dot(normed[l], up_weight[l], nn)
        mlp = mp_sum(jnp.stack([gate_part, up_part]).astype(jnp.bfloat16)).astype(jnp.float32)
        hidden = (jax.nn.gelu(mlp[0], approximate=True) * mlp[1]).astype(jnp.bfloat16)
        target.append(dot(hidden, down_weight[l], nn))
    partial_first = dot(active[0], decoder[0], nn) - target[0]
    partial_second = (
        dot(active[0], decoder[1], nn) + dot(active[1], decoder[2], nn) - target[1]
    )
    loss_scale = 1.0 / math.sqrt(tokens)
    errors = [gather_outer(sum_tokens(partial_first, 0), 0, 0), gather_outer(sum_tokens(partial_second, 1), 1, 0)]
    grad_decoder = decoder_gradient([active[0]], errors[0], loss_scale, (0,))
    back_first = lax.optimization_barrier(dot(errors[0], decoder[0], nt))
    back_first = back_first + dot(errors[1], decoder[1], nt)
    back_second = dot(errors[1], decoder[2], nt)
    own = jnp.stack([back_first, back_second]).astype(jnp.bfloat16)
    *inner, last = bits_of("mp")
    for bit in inner:
        own = own + swap(own, "mp", bit)
    received = swap(own, "mp", last)
    grad_decoder = decoder_gradient(active, errors[1], loss_scale, (1, 2), grad_decoder)
    grad_encoder, grad_bias = encoder_gradient(active, own, received, normed, loss_scale)
    return (grad_encoder, grad_bias, grad_decoder)


def solution(mesh):
    return jax.shard_map(
        body,
        mesh=mesh,
        in_specs=(
            P(None, "feat", "mp"),
            P(None, "mp"),
            P(None, "mp", "feat"),
            P(None, "mp", "feat"),
            P(None, "feat", "mp"),
            P(None, "feat", "mp"),
            P(None, "feat"),
            P(None, "feat", "mp"),
        ),
        out_specs=(P(None, "feat", "mp"), P(None, "feat"), P(None, "feat", "mp")),
        check_vma=False,
    )
```

```python
import math

import jax
import jax.numpy as jnp
from jax import lax
from jax.experimental import pallas as pl
from jax.experimental.pallas import tpu as pltpu
from jax.sharding import PartitionSpec as P


D = 2304


sparsity_weight = 0.1


def swap(values, axis, bit):
    size = lax.axis_size(axis)
    return lax.ppermute(values, axis, [(i, i ^ bit) for i in range(size)])


def bits_of(axis):
    size = lax.axis_size(axis)
    return [1 << k for k in range(size.bit_length() - 1)]


def mp_sum(values):
    for bit in bits_of("mp"):
        values = values + swap(values, "mp", bit)
    return values


def join(*parts):
    return jnp.concatenate(parts, axis=0)


def gather_inner(block):
    place = lax.axis_index("feat")
    bits = bits_of("feat")[2:]
    if len(bits) != 2:
        for bit in reversed(bits):
            other = swap(block, "feat", bit)
            upper = (place & bit) > 0
            block = join(jnp.where(upper, other, block), jnp.where(upper, block, other))
        return block
    low, high = bits
    far, both, near = (swap(block, "feat", b) for b in (high, high | low, low))
    at_low, at_high = (place & low) > 0, (place & high) > 0

    def pick(l, h):
        same_low = jnp.where(at_high == h, block, far)
        other_low = jnp.where(at_high == h, near, both)
        return jnp.where(at_low == l, same_low, other_low)

    return join(pick(False, False), pick(False, True), pick(True, False), pick(True, True))


def stack_rows(upper, lower, flops):
    rows, cols = upper.shape

    def kernel(upper_ref, lower_ref, out_ref):
        out_ref[:rows] = upper_ref[...]
        out_ref[rows:] = lower_ref[...]

    return pl.pallas_call(
        kernel,
        out_shape=jax.ShapeDtypeStruct((2 * rows, cols), upper.dtype),
        in_specs=[pl.BlockSpec(memory_space=pltpu.VMEM)] * 2,
        out_specs=pl.BlockSpec(memory_space=pltpu.VMEM),
        compiler_params=pltpu.CompilerParams(vmem_limit_bytes=4 << 20),
        cost_estimate=pl.CostEstimate(flops=flops, bytes_accessed=1 << 16, transcendentals=0),
    )(upper, lower)


def gather_outer(quarter, layer, flops):
    rows = quarter.shape[0]
    near, far = ((2, 1), (1, 2))[layer]
    across = swap(quarter, "feat", near)
    half = stack_rows(quarter, across, flops) if flops else join(quarter, across)
    other = swap(half, "feat", far)
    if layer == 0:
        return join(half, other)
    return join(quarter, other[:rows], across, other[rows:])


def send_add(kept, sent, bit):
    return kept + swap(sent.astype(jnp.bfloat16), "feat", bit).astype(jnp.float32)


def sum_tokens(values, layer):
    rows = values.shape[0] // 4
    own, second, first, both = (values[k * rows : (k + 1) * rows] for k in range(4))
    if layer == 0:
        half = send_add(values[: 2 * rows], values[2 * rows :], 1)
        quarter = send_add(half[:rows], half[rows:], 2)
    else:
        half = send_add(join(own, first), join(second, both), 2)
        quarter = send_add(half[:rows], half[rows:], 1)
    bits = bits_of("feat")[2:]
    if len(bits) == 2:
        sent = quarter.astype(jnp.bfloat16)
        offsets = (bits[1], bits[0] | bits[1], bits[0])
        received = [swap(sent, "feat", b) for b in offsets]
        for other in received[:-1]:
            quarter = quarter + other.astype(jnp.float32)
        return add_round(quarter, received[-1], int(4e10))
    for bit in bits:
        received = swap(quarter.astype(jnp.bfloat16), "feat", bit)
        quarter = quarter + received.astype(jnp.float32)
    return quarter.astype(jnp.bfloat16)


def square_sums(values, flops):
    def kernel(values_ref, out_ref):
        v = values_ref[...].astype(jnp.float32)
        out_ref[...] = jnp.sum(v * v, axis=2, keepdims=True)

    return pl.pallas_call(
        kernel,
        out_shape=jax.ShapeDtypeStruct((*values.shape[:2], 1), jnp.float32),
        in_specs=[pl.BlockSpec(memory_space=pltpu.VMEM)],
        out_specs=pl.BlockSpec(memory_space=pltpu.VMEM),
        compiler_params=pltpu.CompilerParams(vmem_limit_bytes=4 << 20),
        cost_estimate=pl.CostEstimate(flops=flops, bytes_accessed=1 << 16, transcendentals=0),
    )(values)


def normalize(values, inverse_rms, gain, flops):
    layers, rows, cols = values.shape

    def kernel(values_ref, inverse_ref, gain_ref, out_ref):
        for l in range(layers):
            scaled = values_ref[l].astype(jnp.float32) * inverse_ref[l] * gain_ref[l : l + 1]
            out_ref[:, l * cols : (l + 1) * cols] = scaled.astype(jnp.bfloat16)

    return pl.pallas_call(
        kernel,
        out_shape=jax.ShapeDtypeStruct((rows, layers * cols), jnp.bfloat16),
        in_specs=[pl.BlockSpec(memory_space=pltpu.VMEM)] * 3,
        out_specs=pl.BlockSpec(memory_space=pltpu.VMEM),
        compiler_params=pltpu.CompilerParams(vmem_limit_bytes=4 << 20),
        cost_estimate=pl.CostEstimate(flops=flops, bytes_accessed=1 << 16, transcendentals=0),
    )(values, inverse_rms, gain)


def add_round(kept, received, flops):
    def kernel(kept_ref, received_ref, out_ref):
        total = kept_ref[...] + received_ref[...].astype(jnp.float32)
        out_ref[...] = total.astype(jnp.bfloat16)

    return pl.pallas_call(
        kernel,
        out_shape=jax.ShapeDtypeStruct(kept.shape, jnp.bfloat16),
        in_specs=[pl.BlockSpec(memory_space=pltpu.VMEM)] * 2,
        out_specs=pl.BlockSpec(memory_space=pltpu.VMEM),
        compiler_params=pltpu.CompilerParams(vmem_limit_bytes=4 << 20),
        cost_estimate=pl.CostEstimate(flops=flops, bytes_accessed=1 << 16, transcendentals=0),
    )(kept, received)


def row_chunks(rows, most):
    size = min(rows, most)
    while rows % size:
        size //= 2
    return [(at, size) for at in range(0, rows, size)]


def dot(a, b, contract):
    return lax.dot_general(a, b, (contract, ((), ())), preferred_element_type=jnp.float32)


tn = ((0,), (0,))
nn = ((1,), (0,))
nt = ((1,), (1,))


def decoder_gradient(lefts, right, scale, slots, into=None):
    tokens, features = lefts[0].shape
    cols = right.shape[1]
    count = len(lefts)
    chunks = row_chunks(features, 256)

    def kernel(*refs):
        left_refs, right_ref = refs[:count], refs[count]
        out_ref, held, sems = refs[-3:]
        right_value = right_ref[...]
        copies = []
        for k, left_ref in enumerate(left_refs):
            for c, (at, size) in enumerate(chunks):
                rows = pl.ds(at, size)
                held[k, rows] = (scale * dot(left_ref[:, rows], right_value, tn)).astype(jnp.bfloat16)
                target = out_ref.at[slots[k], rows]
                copies.append(pltpu.make_async_copy(held.at[k, rows], target, sems.at[k, c]))
                copies[-1].start()
        for copy in copies:
            copy.wait()

    vmem = pl.BlockSpec(memory_space=pltpu.VMEM)
    hbm = pl.BlockSpec(memory_space=pl.ANY)
    more = () if into is None else (into,)
    return pl.pallas_call(
        kernel,
        out_shape=jax.ShapeDtypeStruct((3, features, cols), jnp.bfloat16),
        in_specs=[vmem] * (count + 1) + [hbm] * len(more),
        out_specs=hbm,
        input_output_aliases={count + 1: 0} if more else {},
        scratch_shapes=[
            pltpu.VMEM((count, features, cols), jnp.bfloat16),
            pltpu.SemaphoreType.DMA((count, len(chunks))),
        ],
        compiler_params=pltpu.CompilerParams(vmem_limit_bytes=(8 + 8 * count) << 20),
        cost_estimate=pl.CostEstimate(
            flops=2 * count * tokens * features * cols,
            bytes_accessed=2 * count * features * cols,
            transcendentals=0,
        ),
    )(*lefts, right, *more)


def encoder_gradient(active, own, received, normed, scale):
    tokens, features = active[0].shape
    cols = normed[0].shape[1]
    chunks = row_chunks(features, 256)

    def kernel(active_0, active_1, own_ref, received_ref, normed_0, normed_1, out_ref, bias_ref, held, sems):
        copies = []
        for l, (active_ref, normed_ref) in enumerate(((active_0, normed_0), (active_1, normed_1))):
            right = normed_ref[...]
            for c, (at, size) in enumerate(chunks):
                rows = pl.ds(at, size)
                backward = own_ref[l, :, rows].astype(jnp.float32) + received_ref[l, :, rows].astype(jnp.float32)
                open_gate = active_ref[:, rows].astype(jnp.float32) > 0
                pre_grad = jnp.where(open_gate, scale * (backward + sparsity_weight), 0.0).astype(jnp.bfloat16)
                bias_ref[l : l + 1, rows] = jnp.sum(pre_grad.astype(jnp.float32), axis=0, keepdims=True)
                held[l, rows] = dot(pre_grad, right, tn).astype(jnp.bfloat16)
                copies.append(pltpu.make_async_copy(held.at[l, rows], out_ref.at[l, rows], sems.at[l, c]))
                copies[-1].start()
        for copy in copies:
            copy.wait()

    vmem = pl.BlockSpec(memory_space=pltpu.VMEM)
    return pl.pallas_call(
        kernel,
        out_shape=(
            jax.ShapeDtypeStruct((2, features, cols), jnp.bfloat16),
            jax.ShapeDtypeStruct((2, features), jnp.float32),
        ),
        in_specs=[vmem] * 6,
        out_specs=(pl.BlockSpec(memory_space=pl.ANY), vmem),
        scratch_shapes=[
            pltpu.VMEM((2, features, cols), jnp.bfloat16),
            pltpu.SemaphoreType.DMA((2, len(chunks))),
        ],
        compiler_params=pltpu.CompilerParams(vmem_limit_bytes=24 << 20),
        cost_estimate=pl.CostEstimate(
            flops=4 * tokens * features * cols, bytes_accessed=4 * features * cols, transcendentals=0
        ),
    )(*active, own, received, *normed)


def body(residual, norm_gain, gate_weight, up_weight, down_weight, encoder, encoder_bias, decoder):
    squares = mp_sum(square_sums(residual, int(1e10)))
    inverse_rms = lax.rsqrt(squares / D + 1e-06)
    model_cols = decoder.shape[2]
    quarter = gather_inner(normalize(residual, inverse_rms, norm_gain, int(4e10)))
    normed = [
        gather_outer(quarter[:, l * model_cols : (l + 1) * model_cols], l, int(1e10) if l == 0 else int(1e6))
        for l in range(2)
    ]
    tokens = normed[0].shape[0]
    active = []
    target = []
    for l in range(2):
        preact = mp_sum(dot(normed[l], encoder[l], nt))
        active.append(jnp.maximum(preact + encoder_bias[l][None, :], 0.0).astype(jnp.bfloat16))
        gate_part = dot(normed[l], gate_weight[l], nn)
        up_part = dot(normed[l], up_weight[l], nn)
        mlp = mp_sum(jnp.stack([gate_part, up_part]).astype(jnp.bfloat16)).astype(jnp.float32)
        hidden = (jax.nn.gelu(mlp[0], approximate=True) * mlp[1]).astype(jnp.bfloat16)
        target.append(dot(hidden, down_weight[l], nn))
    partial_first = dot(active[0], decoder[0], nn) - target[0]
    partial_second = (
        dot(active[0], decoder[1], nn) + dot(active[1], decoder[2], nn) - target[1]
    )
    loss_scale = 1.0 / math.sqrt(tokens)
    errors = [gather_outer(sum_tokens(partial_first, 0), 0, 0), gather_outer(sum_tokens(partial_second, 1), 1, 0)]
    grad_decoder = decoder_gradient([active[0]], errors[0], loss_scale, (0,))
    back_first = lax.optimization_barrier(dot(errors[0], decoder[0], nt))
    back_first = back_first + dot(errors[1], decoder[1], nt)
    back_second = dot(errors[1], decoder[2], nt)
    own = jnp.stack([back_first, back_second]).astype(jnp.bfloat16)
    *inner, last = bits_of("mp")
    for bit in inner:
        own = own + swap(own, "mp", bit)
    received = swap(own, "mp", last)
    grad_decoder = decoder_gradient(active, errors[1], loss_scale, (1, 2), grad_decoder)
    grad_encoder, grad_bias = encoder_gradient(active, own, received, normed, loss_scale)
    return (grad_encoder, grad_bias, grad_decoder)


def solution(mesh):
    return jax.shard_map(
        body,
        mesh=mesh,
        in_specs=(
            P(None, "feat", "mp"),
            P(None, "mp"),
            P(None, "mp", "feat"),
            P(None, "mp", "feat"),
            P(None, "feat", "mp"),
            P(None, "feat", "mp"),
            P(None, "feat"),
            P(None, "feat", "mp"),
        ),
        out_specs=(P(None, "feat", "mp"), P(None, "feat"), P(None, "feat", "mp")),
        check_vma=False,
    )
```

```python
import math

import jax
import jax.numpy as jnp
from jax import lax
from jax.experimental import pallas as pl
from jax.experimental.pallas import tpu as pltpu
from jax.sharding import PartitionSpec as P


D = 2304


sparsity_weight = 0.1


def swap(values, axis, bit):
    size = lax.axis_size(axis)
    return lax.ppermute(values, axis, [(i, i ^ bit) for i in range(size)])


def bits_of(axis):
    size = lax.axis_size(axis)
    return [1 << k for k in range(size.bit_length() - 1)]


def mp_sum(values):
    for bit in bits_of("mp"):
        values = values + swap(values, "mp", bit)
    return values


def join(*parts):
    return jnp.concatenate(parts, axis=0)


def gather_inner(block):
    place = lax.axis_index("feat")
    bits = bits_of("feat")[2:]
    if len(bits) != 2:
        for bit in reversed(bits):
            other = swap(block, "feat", bit)
            upper = (place & bit) > 0
            block = join(jnp.where(upper, other, block), jnp.where(upper, block, other))
        return block
    low, high = bits
    far, both, near = (swap(block, "feat", b) for b in (high, high | low, low))
    at_low, at_high = (place & low) > 0, (place & high) > 0

    def pick(l, h):
        same_low = jnp.where(at_high == h, block, far)
        other_low = jnp.where(at_high == h, near, both)
        return jnp.where(at_low == l, same_low, other_low)

    return join(pick(False, False), pick(False, True), pick(True, False), pick(True, True))


def stack_rows(upper, lower, flops):
    rows, cols = upper.shape

    def kernel(upper_ref, lower_ref, out_ref):
        out_ref[:rows] = upper_ref[...]
        out_ref[rows:] = lower_ref[...]

    return pl.pallas_call(
        kernel,
        out_shape=jax.ShapeDtypeStruct((2 * rows, cols), upper.dtype),
        in_specs=[pl.BlockSpec(memory_space=pltpu.VMEM)] * 2,
        out_specs=pl.BlockSpec(memory_space=pltpu.VMEM),
        compiler_params=pltpu.CompilerParams(vmem_limit_bytes=4 << 20),
        cost_estimate=pl.CostEstimate(flops=flops, bytes_accessed=1 << 16, transcendentals=0),
    )(upper, lower)


def gather_outer(quarter, layer, flops):
    rows = quarter.shape[0]
    near, far = ((2, 1), (1, 2))[layer]
    across = swap(quarter, "feat", near)
    half = stack_rows(quarter, across, flops) if flops else join(quarter, across)
    other = swap(half, "feat", far)
    if layer == 0:
        return join(half, other)
    return join(quarter, other[:rows], across, other[rows:])


def send_add(kept, sent, bit):
    return kept + swap(sent.astype(jnp.bfloat16), "feat", bit).astype(jnp.float32)


def sum_tokens(values, layer):
    rows = values.shape[0] // 4
    own, second, first, both = (values[k * rows : (k + 1) * rows] for k in range(4))
    if layer == 0:
        half = send_add(values[: 2 * rows], values[2 * rows :], 1)
        quarter = send_add(half[:rows], half[rows:], 2)
    else:
        half = send_add(join(own, first), join(second, both), 2)
        quarter = send_add(half[:rows], half[rows:], 1)
    bits = bits_of("feat")[2:]
    if len(bits) == 2:
        sent = quarter.astype(jnp.bfloat16)
        offsets = ((bits[1], bits[0] | bits[1], bits[0]), (bits[0], bits[0] | bits[1], bits[1]))[layer]
        received = [swap(sent, "feat", b) for b in offsets]
        for other in received[:-1]:
            quarter = quarter + other.astype(jnp.float32)
        return add_round(quarter, received[-1], int(4e10))
    for bit in bits:
        received = swap(quarter.astype(jnp.bfloat16), "feat", bit)
        quarter = quarter + received.astype(jnp.float32)
    return quarter.astype(jnp.bfloat16)


def square_sums(values, flops):
    def kernel(values_ref, out_ref):
        v = values_ref[...].astype(jnp.float32)
        out_ref[...] = jnp.sum(v * v, axis=2, keepdims=True)

    return pl.pallas_call(
        kernel,
        out_shape=jax.ShapeDtypeStruct((*values.shape[:2], 1), jnp.float32),
        in_specs=[pl.BlockSpec(memory_space=pltpu.VMEM)],
        out_specs=pl.BlockSpec(memory_space=pltpu.VMEM),
        compiler_params=pltpu.CompilerParams(vmem_limit_bytes=4 << 20),
        cost_estimate=pl.CostEstimate(flops=flops, bytes_accessed=1 << 16, transcendentals=0),
    )(values)


def normalize(values, inverse_rms, gain, flops):
    layers, rows, cols = values.shape

    def kernel(values_ref, inverse_ref, gain_ref, out_ref):
        for l in range(layers):
            scaled = values_ref[l].astype(jnp.float32) * inverse_ref[l] * gain_ref[l : l + 1]
            out_ref[:, l * cols : (l + 1) * cols] = scaled.astype(jnp.bfloat16)

    return pl.pallas_call(
        kernel,
        out_shape=jax.ShapeDtypeStruct((rows, layers * cols), jnp.bfloat16),
        in_specs=[pl.BlockSpec(memory_space=pltpu.VMEM)] * 3,
        out_specs=pl.BlockSpec(memory_space=pltpu.VMEM),
        compiler_params=pltpu.CompilerParams(vmem_limit_bytes=4 << 20),
        cost_estimate=pl.CostEstimate(flops=flops, bytes_accessed=1 << 16, transcendentals=0),
    )(values, inverse_rms, gain)


def add_round(kept, received, flops):
    def kernel(kept_ref, received_ref, out_ref):
        total = kept_ref[...] + received_ref[...].astype(jnp.float32)
        out_ref[...] = total.astype(jnp.bfloat16)

    return pl.pallas_call(
        kernel,
        out_shape=jax.ShapeDtypeStruct(kept.shape, jnp.bfloat16),
        in_specs=[pl.BlockSpec(memory_space=pltpu.VMEM)] * 2,
        out_specs=pl.BlockSpec(memory_space=pltpu.VMEM),
        compiler_params=pltpu.CompilerParams(vmem_limit_bytes=4 << 20),
        cost_estimate=pl.CostEstimate(flops=flops, bytes_accessed=1 << 16, transcendentals=0),
    )(kept, received)


def row_chunks(rows, most):
    size = min(rows, most)
    while rows % size:
        size //= 2
    return [(at, size) for at in range(0, rows, size)]


def dot(a, b, contract):
    return lax.dot_general(a, b, (contract, ((), ())), preferred_element_type=jnp.float32)


tn = ((0,), (0,))
nn = ((1,), (0,))
nt = ((1,), (1,))


def decoder_gradient(lefts, rights, pieces, scale, into=None):
    tokens, features = lefts[0].shape
    cols = rights[0].shape[1]
    count = len(lefts) + len(rights)
    tiles = [
        (a, e, slot, first + at, size)
        for a, e, slot, first, rows in pieces
        for at, size in row_chunks(rows, 256)
    ]
    total = sum(size for *_, size in tiles)

    def kernel(*refs):
        left_refs, right_refs = refs[: len(lefts)], refs[len(lefts) : count]
        out_ref, held, sems = refs[-3:]
        copies = []
        place = 0
        for k, (a, e, slot, at, size) in enumerate(tiles):
            rows, kept = pl.ds(at, size), pl.ds(place, size)
            value = scale * dot(left_refs[a][:, rows], right_refs[e][...], tn)
            held[kept] = value.astype(jnp.bfloat16)
            copies.append(pltpu.make_async_copy(held.at[kept], out_ref.at[slot, rows], sems.at[k]))
            copies[-1].start()
            place += size
        for copy in copies:
            copy.wait()

    vmem = pl.BlockSpec(memory_space=pltpu.VMEM)
    hbm = pl.BlockSpec(memory_space=pl.ANY)
    more = () if into is None else (into,)
    return pl.pallas_call(
        kernel,
        out_shape=jax.ShapeDtypeStruct((3, features, cols), jnp.bfloat16),
        in_specs=[vmem] * count + [hbm] * len(more),
        out_specs=hbm,
        input_output_aliases={count: 0} if more else {},
        scratch_shapes=[
            pltpu.VMEM((total, cols), jnp.bfloat16),
            pltpu.SemaphoreType.DMA((len(tiles),)),
        ],
        compiler_params=pltpu.CompilerParams(vmem_limit_bytes=28 << 20),
        cost_estimate=pl.CostEstimate(
            flops=2 * tokens * total * cols, bytes_accessed=2 * total * cols, transcendentals=0
        ),
    )(*lefts, *rights, *more)


def encoder_gradient(active, own, received, normed, scale):
    tokens, features = active[0].shape
    cols = normed[0].shape[1]
    chunks = row_chunks(features, 256)

    def kernel(active_0, active_1, own_ref, received_ref, normed_0, normed_1, out_ref, bias_ref, held, sems):
        copies = []
        for l, (active_ref, normed_ref) in enumerate(((active_0, normed_0), (active_1, normed_1))):
            right = normed_ref[...]
            for c, (at, size) in enumerate(chunks):
                rows = pl.ds(at, size)
                backward = own_ref[l, :, rows].astype(jnp.float32) + received_ref[l, :, rows].astype(jnp.float32)
                open_gate = active_ref[:, rows].astype(jnp.float32) > 0
                pre_grad = jnp.where(open_gate, scale * (backward + sparsity_weight), 0.0).astype(jnp.bfloat16)
                bias_ref[l : l + 1, rows] = jnp.sum(pre_grad.astype(jnp.float32), axis=0, keepdims=True)
                held[l, rows] = dot(pre_grad, right, tn).astype(jnp.bfloat16)
                copies.append(pltpu.make_async_copy(held.at[l, rows], out_ref.at[l, rows], sems.at[l, c]))
                copies[-1].start()
        for copy in copies:
            copy.wait()

    vmem = pl.BlockSpec(memory_space=pltpu.VMEM)
    return pl.pallas_call(
        kernel,
        out_shape=(
            jax.ShapeDtypeStruct((2, features, cols), jnp.bfloat16),
            jax.ShapeDtypeStruct((2, features), jnp.float32),
        ),
        in_specs=[vmem] * 6,
        out_specs=(pl.BlockSpec(memory_space=pl.ANY), vmem),
        scratch_shapes=[
            pltpu.VMEM((2, features, cols), jnp.bfloat16),
            pltpu.SemaphoreType.DMA((2, len(chunks))),
        ],
        compiler_params=pltpu.CompilerParams(vmem_limit_bytes=24 << 20),
        cost_estimate=pl.CostEstimate(
            flops=4 * tokens * features * cols, bytes_accessed=4 * features * cols, transcendentals=0
        ),
    )(*active, own, received, *normed)


def body(residual, norm_gain, gate_weight, up_weight, down_weight, encoder, encoder_bias, decoder):
    squares = mp_sum(square_sums(residual, int(1e10)))
    inverse_rms = lax.rsqrt(squares / D + 1e-06)
    model_cols = decoder.shape[2]
    quarter = gather_inner(normalize(residual, inverse_rms, norm_gain, int(4e10)))
    normed = [
        gather_outer(quarter[:, l * model_cols : (l + 1) * model_cols], l, int(1e10) if l == 0 else int(1e6))
        for l in range(2)
    ]
    tokens = normed[0].shape[0]
    active = []
    target = []
    for l in range(2):
        preact = mp_sum(dot(normed[l], encoder[l], nt))
        active.append(jnp.maximum(preact + encoder_bias[l][None, :], 0.0).astype(jnp.bfloat16))
        gate_part = dot(normed[l], gate_weight[l], nn)
        up_part = dot(normed[l], up_weight[l], nn)
        mlp = mp_sum(jnp.stack([gate_part, up_part]).astype(jnp.bfloat16)).astype(jnp.float32)
        hidden = (jax.nn.gelu(mlp[0], approximate=True) * mlp[1]).astype(jnp.bfloat16)
        target.append(dot(hidden, down_weight[l], nn))
    partial_first = dot(active[0], decoder[0], nn) - target[0]
    partial_second = (
        dot(active[0], decoder[1], nn) + dot(active[1], decoder[2], nn) - target[1]
    )
    loss_scale = 1.0 / math.sqrt(tokens)
    errors = [gather_outer(sum_tokens(partial_first, 0), 0, 0), gather_outer(sum_tokens(partial_second, 1), 1, 0)]
    features = decoder.shape[1]
    early = features // 4
    grad_decoder = decoder_gradient(active[:1], errors[:1], [(0, 0, 0, 0, early)], loss_scale)
    back_first = lax.optimization_barrier(dot(errors[0], decoder[0], nt))
    back_first = back_first + dot(errors[1], decoder[1], nt)
    back_second = dot(errors[1], decoder[2], nt)
    own = jnp.stack([back_first, back_second]).astype(jnp.bfloat16)
    *inner, last = bits_of("mp")
    for bit in inner:
        own = own + swap(own, "mp", bit)
    received = swap(own, "mp", last)
    rest = [(0, 0, 0, early, features - early), (0, 1, 1, 0, features), (1, 1, 2, 0, features)]
    grad_decoder = decoder_gradient(active, errors, rest, loss_scale, grad_decoder)
    grad_encoder, grad_bias = encoder_gradient(active, own, received, normed, loss_scale)
    return (grad_encoder, grad_bias, grad_decoder)


def solution(mesh):
    return jax.shard_map(
        body,
        mesh=mesh,
        in_specs=(
            P(None, "feat", "mp"),
            P(None, "mp"),
            P(None, "mp", "feat"),
            P(None, "mp", "feat"),
            P(None, "feat", "mp"),
            P(None, "feat", "mp"),
            P(None, "feat"),
            P(None, "feat", "mp"),
        ),
        out_specs=(P(None, "feat", "mp"), P(None, "feat"), P(None, "feat", "mp")),
        check_vma=False,
    )
```
